32 devices in a mesh: row: 4 (over y, x), col: 8 (over z, core).
Axes of the slice: x: 2, y: 2, z: 4, core: 2. Of those that a mesh axis runs over, the one named last changes fastest.
Arguments:
- left_matrix: bfloat16 [3072, 32768], P('row', 'col'), may hold values from -6 to 6
- right_matrix: bfloat16 [32768, 4096], P('row', 'col'), may hold values from -0.0546875 to 0.0546875
- left_mask: int32 [24, 256], P('row', 'col'), may hold values from 0 to 1
- right_mask: int32 [256, 32], P('row', 'col'), may hold values from 0 to 1
- keep_mask: int32 [24, 32], P('row', 'col'), may hold values 0 or 1
Outputs:
- product: bfloat16 [3072, 4096], P('row', 'col')
The draws below stay inside these ranges and needn't reach their ends.
All inputs are finite; a program needn't handle non-finite values. No bound on the sum of `keep_mask` on one device may be relied on, other than what follows from the above.
Results may differ from the reference program's by a relative error of at most 0.001.
Values may be sent and summed in bfloat16 or wider, within the bound.
A program may use at most 128 MiB of HBM per device.

```python
import jax
import jax.numpy as jnp

ORDER = 32768
BLOCK = 128
TICKS = 3
MR_DEV = 768
NC_DEV = 512
M = 3072
N = 4096
MB = 24
KB = 256
NB = 32
UNIT = 8192
N_ROW = 4


def banded(key, rows, cols):
    row_pos = jnp.arange(rows, dtype=jnp.int32)[:, None]
    col_pos = jnp.arange(cols, dtype=jnp.int32)[None, :]
    centre = row_pos * cols // rows
    distance = jnp.abs(col_pos - centre)
    distance = jnp.minimum(distance, cols - distance)
    width = max(cols // 8, 1)
    threshold = 250 + 700 * jnp.maximum(width - distance, 0) // width
    rolled = jax.random.randint(key, (rows, cols), 0, 1000)
    return (rolled < threshold).astype(jnp.int32)


def draw_left_mask(key, part):
    return banded(jax.random.fold_in(key, 11), MB, KB)


def draw_right_mask(key, part):
    return banded(jax.random.fold_in(key, 23), NB, KB).T


def with_ends(result, own_key, low, largest):
    place = [jax.random.randint(jax.random.fold_in(own_key, axis), (), 0, length) for axis, length in enumerate(result.shape)]
    main_axis = result.shape.index(max(result.shape))
    beside = place[:main_axis] + [(place[main_axis] + 1) % result.shape[main_axis]] + place[main_axis + 1:]
    return result.at[tuple(place)].set(low).at[tuple(beside)].set(largest)


def level_of(own_key, extent, cuts, low, largest):
    level, own = 1.0, jax.random.fold_in(own_key, 6)
    for position, shards_of in cuts:
        draws = jnp.exp(jax.random.uniform(jax.random.fold_in(own, position), (shards_of,), jnp.float32, low / len(cuts), largest / len(cuts)))
        level = level * jnp.repeat(draws, extent[position] // shards_of).reshape([-1 if axis == position else 1 for axis in range(len(extent))])
    return level


def gaussian(key, extent, deviation, bound, cuts=(), kind=jnp.bfloat16):
    factor_of = level_of(key, extent, cuts, -0.22, 0.18) if cuts else 1.0
    result = jax.random.normal(key, extent, jnp.float32) * deviation * factor_of
    return jnp.minimum(jnp.maximum(result, -bound), bound).astype(kind)


def setup_inputs(seed: int = 0) -> dict:
    arg_keys = jax.random.split(jax.random.key(seed), 6)
    left_matrix = gaussian(arg_keys[0], (M, ORDER), 1.0, 6.0, ((0, 4), (1, 8)))
    right_matrix = gaussian(arg_keys[1], (ORDER, N), (TICKS * UNIT // 2) ** -0.5, 0.0546875, ((0, 4), (1, 8)))
    left_mask = draw_left_mask(jax.random.fold_in(arg_keys[5], 71), 0)
    right_mask = draw_right_mask(jax.random.fold_in(arg_keys[5], 71), 0)
    keep_mask = with_ends((jax.random.randint(arg_keys[4], (MB, NB), 0, 4) < 3).astype(jnp.int32), jax.random.fold_in(arg_keys[4], 1), 0, 1)
    return {"left_matrix": left_matrix, "right_matrix": right_matrix, "left_mask": left_mask, "right_mask": right_mask, "keep_mask": keep_mask}


def sparsify(matrix, mask):
    rows, cols = matrix.shape
    shaped = matrix.reshape(rows // BLOCK, BLOCK, cols // BLOCK, BLOCK)
    return (shaped * mask[:, None, :, None].astype(matrix.dtype)).reshape(rows, cols)


def reference(left_matrix, right_matrix, left_mask, right_mask, keep_mask):
    left_sparse = sparsify(left_matrix, left_mask)
    right_sparse = sparsify(right_matrix, right_mask)
    group_cols = 2 * NC_DEV
    panels = []
    for panel in range(N_ROW):
        pieces = []
        for group in range(N_ROW):
            total = jnp.zeros((MR_DEV, group_cols), jnp.float32)
            for tick in range(TICKS):
                unit = (panel + group + tick) % N_ROW
                left_piece = left_sparse[panel * MR_DEV:(panel + 1) * MR_DEV, unit * UNIT:(unit + 1) * UNIT]
                right_piece = right_sparse[unit * UNIT:(unit + 1) * UNIT, group * group_cols:(group + 1) * group_cols]
                total = total + jnp.dot(left_piece, right_piece, preferred_element_type=jnp.float32)
            pieces.append(total)
        panels.append(jnp.concatenate(pieces, axis=1))
    total_all = jnp.concatenate(panels, axis=0)
    kept = total_all.reshape(MB, BLOCK, NB, BLOCK) * keep_mask[:, None, :, None].astype(jnp.float32)
    return kept.reshape(M, N).astype(jnp.bfloat16)
```

```python
import functools

import jax
import jax.numpy as jnp
from jax import lax
from jax.experimental import pallas as pl
from jax.experimental.pallas import tpu as pltpu
from jax.sharding import PartitionSpec as P

BLOCK = 128
TICKS = 3


def passed_along(value, axis, by):
    length = lax.axis_size(axis)
    return lax.ppermute(value, axis, [(i, (i + by) % length) for i in range(length)])


def partner(block, axis, stride):
    count = lax.axis_size(axis)
    route = []
    for low in range(count):
        high = low | 1 << stride
        if high != low and high < count:
            route += [(low, high), (high, low)]
    return lax.ppermute(block, axis, route)


def sparsify(matrix, mask):
    rows, cols = matrix.shape
    shaped = matrix.reshape(rows // BLOCK, BLOCK, cols // BLOCK, BLOCK)
    return (shaped * mask[:, None, :, None].astype(matrix.dtype)).reshape(rows, cols)


def shards(left_matrix, right_matrix, left_mask, right_mask, keep_mask):
    row_index = lax.axis_index("row")
    col_index = lax.axis_index("col")
    group = col_index // 2
    parity = col_index % 2
    levels = lax.axis_size("row").bit_length() - 1
    left_sparse = sparsify(left_matrix, left_mask)
    right_sparse = sparsify(right_matrix, right_mask)

    def join(own, other):
        lower = jnp.where(parity == 0, own, other)
        upper = jnp.where(parity == 0, other, own)
        return jnp.concatenate([lower, upper], axis=1)

    for level in range(levels):
        moved = passed_along(right_sparse, "row", -(1 << level))
        right_sparse = jnp.where((group >> level) % 2 == 1, moved, right_sparse)
    holding = left_sparse
    for level in range(levels):
        moved = passed_along(holding, "col", -(2 << level))
        holding = jnp.where((row_index >> level) % 2 == 1, moved, holding)

    def whole(state):
        return join(state, partner(state, "col", 0))

    total = jnp.dot(whole(holding), right_sparse, preferred_element_type=jnp.float32)
    for tick in range(1, TICKS):
        holding = passed_along(holding, "col", -2)
        right_sparse = passed_along(right_sparse, "row", -1)
        total = total + jnp.dot(whole(holding), right_sparse, preferred_element_type=jnp.float32)
    rows, cols = total.shape
    kept = total.reshape(rows // BLOCK, BLOCK, cols // BLOCK, BLOCK) * keep_mask[
        :, None, :, None
    ].astype(jnp.float32)
    return kept.reshape(rows, cols).astype(jnp.bfloat16)


LEFT_PIECES = 4
RIGHT_PIECES = 4
SUM_PIECES = 4


def product_kernel(lsrc, rsrc, out, lbuf, rbuf, acc, core_sum, far_sum, loc, y_l, y_r, x_own, x_fwd, z_one, z_two, swap, sums):
    r, c = lax.axis_index("row"), lax.axis_index("col")
    y, x = r // 2, lax.rem(r, 2)
    z, p = c // 2, lax.rem(c, 2)
    rows, half = lbuf.shape[2:]
    width = rbuf.shape[3]
    lrows, rrows, srows = rows // LEFT_PIECES, half // RIGHT_PIECES, rows // SUM_PIECES
    ring = lbuf.shape[1]

    def device(dy, dx, dz, core):
        ny = 1 - y if dy else y
        nx = 1 - x if dx else x
        return (ny * 2 + nx, lax.rem(z + dz + ring, ring) * 2 + core)

    def unit_of(dy, dx):
        return (1 - y if dy else y) * 2 + (1 - x if dx else x)

    def copy(src, dst, sems, index, to):
        send, recv = sems
        return pltpu.make_async_remote_copy(
            src_ref=src, dst_ref=dst, send_sem=send.at[index], recv_sem=recv.at[index],
            device_id=to, device_id_type=pl.DeviceIdType.MESH)

    def arrived(dst, sems, index):
        copy(dst, dst, sems, index, device(0, 0, 0, 1 - p)).wait_recv()

    def used(panel, unit):
        return lax.rem(unit - (x + 2 * panel) - z + 2 * ring, ring) < TICKS

    barrier = pltpu.get_barrier_semaphore()
    peers = [device(1, 0, 0, 0), device(1, 0, 0, 1), device(0, 1, 0, 0), device(0, 1, 0, 1),
             device(0, 0, 0, 1 - p), device(0, 0, 1, p), device(0, 0, -1, p)]
    for peer in peers:
        pl.semaphore_signal(barrier, inc=1, device_id=peer, device_id_type=pl.DeviceIdType.MESH)
    pl.semaphore_wait(barrier, len(peers))

    pending = []

    def send(transfer, when=None):
        pending.append((transfer, when))
        if when is None:
            transfer.start()
        else:
            @pl.when(when)
            def _():
                transfer.start()

    def left_at(panel, unit, j):
        return lbuf.at[panel, unit, pl.ds(j * lrows, lrows)]

    def right_at(unit, q, j):
        return rbuf.at[unit, q, pl.ds(j * rrows, rrows)]

    def left_source(part, j):
        return lsrc.at[pl.ds(j * lrows, lrows), pl.ds(pl.multiple_of(part * half, 128), half)]

    def right_source(core, part, j):
        return rsrc.at[pl.ds(pl.multiple_of((core * 2 + part) * half + j * rrows, 128), rrows)]

    first = {}
    first[0, -1] = True
    first[1, -1] = x == 1
    first[0, 1] = x == 1
    first[1, 1] = True

    def first_hop(panel_is_own, j):
        panel = y if panel_is_own else 1 - y
        for d in (-1, 1):
            ok = (panel == (0 if d == -1 else 1)) | (x == 1)
            src = left_source(y, j) if panel_is_own else left_at(panel, z, j)
            n = (0 if d == -1 else 1, 0 if panel_is_own else 1, j)
            sem = (0 if d == -1 else 1, panel, j)
            send(copy(src, left_at(panel, z, j), z_one, sem, device(0, 0, d, p)), ok)

    own_left = [pltpu.make_async_copy(lsrc.at[:, pl.ds(pl.multiple_of(y * half, 128), half)], lbuf.at[y, z], loc.at[0]),
                pltpu.make_async_copy(rsrc.at[pl.ds(pl.multiple_of((p * 2 + y) * half, 128), half)], rbuf.at[r, p], loc.at[1])]
    for j in range(LEFT_PIECES):
        send(copy(left_source(1 - y, j), left_at(y, z, j), y_l, (j,), device(1, 0, 0, p)))
        first_hop(True, j)
        if j < RIGHT_PIECES:
            for core in range(2):
                send(copy(right_source(core, y, j), right_at(r, p, j), x_own, (core, p, j), device(0, 1, 0, core)))
    send(copy(rsrc.at[pl.ds(pl.multiple_of(((1 - p) * 2 + y) * half, 128), half)], rbuf.at[r, p], swap, (0,), device(0, 0, 0, 1 - p)))
    for local in own_left:
        local.start()
    for j in range(RIGHT_PIECES):
        for core in range(2):
            send(copy(right_source(core, 1 - y, j), right_at(r, p, j), y_r, (core, p, j), device(1, 0, 0, core)))

    acc[...] = jnp.zeros_like(acc)

    def one_hop_arrives(panel, d, j):
        unit = lax.rem(z - d + ring, ring)
        ok = (panel == (0 if d == -1 else 1)) | (x == 1)
        @pl.when(ok)
        def _():
            arrived(left_at(panel, unit, j), z_one, (0 if d == -1 else 1, panel, j))
        mine = j < LEFT_PIECES // 2 if d == -1 else j >= LEFT_PIECES // 2
        on = jnp.where(x == 0, panel == (0 if d == -1 else 1), (panel == 0) & mine)
        send(copy(left_at(panel, unit, j), left_at(panel, unit, j), z_two, (panel, j), device(0, 0, d, p)), on)

    for j in range(LEFT_PIECES):
        arrived(left_at(1 - y, z, j), y_l, (j,))
        first_hop(False, j)
        for d in (-1, 1):
            one_hop_arrives(y, d, j)
    behind = unit_of(1, 0)

    for j in range(max(LEFT_PIECES, RIGHT_PIECES)):
        if j < LEFT_PIECES:
            for d in (-1, 1):
                one_hop_arrives(1 - y, d, j)
        if j < RIGHT_PIECES:
            for q in range(2):
                arrived(right_at(behind, q, j), y_r, (p, q, j))
                send(copy(right_at(behind, q, j), right_at(behind, q, j), x_fwd, (q, j), device(0, 1, 0, p)))

    def multiply(panel, unit, start, depth):
        @pl.when(used(panel, unit))
        def _():
            for q in range(2):
                acc[panel, q] += jnp.dot(
                    lbuf[panel, unit, :, start:start + depth], rbuf[unit, q, start:start + depth],
                    preferred_element_type=jnp.float32)

    for local in own_left:
        local.wait()
    arrived(rbuf.at[r, 1 - p], swap, (0,))
    across = unit_of(0, 1)
    for j in range(RIGHT_PIECES):
        for q in range(2):
            arrived(right_at(across, q, j), x_own, (p, q, j))
    opposite = lax.rem(z + 2, ring)
    for panel in range(2):
        for j in range(LEFT_PIECES):
            @pl.when((x == 0) | (panel == 0))
            def _():
                arrived(left_at(panel, opposite, j), z_two, (panel, j))

    def early(panel):
        @pl.loop(0, 3)
        def _(step):
            unit = jnp.where(step == 0, r, jnp.where(step == 1, across, behind))
            multiply(panel, unit, 0, half)

    early(1 - y)
    last = unit_of(1, 1)
    for j in range(RIGHT_PIECES):
        for q in range(2):
            arrived(right_at(last, q, j), x_fwd, (q, j))
        multiply(1 - y, last, j * rrows, rrows)

    def part(ref, j, *index):
        return ref.at[(*index, pl.ds(j * srows, srows))]

    for j in range(SUM_PIECES):
        send(copy(part(acc, j, 1 - y, 1 - p), part(core_sum, j, 0), sums, (0, j), device(0, 0, 0, 1 - p)))
    for j in range(SUM_PIECES):
        piece = pl.ds(j * srows, srows)
        arrived(part(core_sum, j, 0), sums, (0, j))
        acc[1 - y, p, piece] += core_sum[0, piece]
        send(copy(part(acc, j, 1 - y, p), part(far_sum, j), sums, (1, j), device(1, 0, 0, p)))
    early(y)
    multiply(y, last, 0, half)
    for j in range(SUM_PIECES):
        send(copy(part(acc, j, y, 1 - p), part(core_sum, j, 1), sums, (2, j), device(0, 0, 0, 1 - p)))
    for j in range(SUM_PIECES):
        piece = pl.ds(j * srows, srows)
        arrived(part(core_sum, j, 1), sums, (2, j))
        arrived(part(far_sum, j), sums, (1, j))
        out[piece] = acc[y, p, piece] + core_sum[1, piece] + far_sum[piece]

    for transfer, when in pending:
        if when is None:
            transfer.wait_send()
        else:
            @pl.when(when)
            def _():
                transfer.wait_send()


def kernel_entry(sems, lsrc, rsrc, out, lbuf, rbuf, acc, core_sum, far_sum, loc, *rest):
    pairs = [(rest[2 * i], rest[2 * i + 1]) for i in range(sems)]
    product_kernel(lsrc, rsrc, out, lbuf, rbuf, acc, core_sum, far_sum, loc, *pairs)


def split_shards(left_matrix, right_matrix, left_mask, right_mask, keep_mask):
    left_sparse = sparsify(left_matrix, left_mask)
    right_sparse = sparsify(right_matrix, right_mask)
    rows, depth = left_matrix.shape
    width = right_matrix.shape[1]
    half = depth // 2
    units = lax.axis_size("row")
    shapes = [(LEFT_PIECES,), (2, 2, RIGHT_PIECES), (2, 2, RIGHT_PIECES), (2, RIGHT_PIECES),
              (2, 2, LEFT_PIECES), (2, LEFT_PIECES), (1,), (3, SUM_PIECES)]
    sems = [pltpu.SemaphoreType.DMA(shape) for shape in shapes for _ in range(2)]
    total = pl.pallas_call(
        functools.partial(kernel_entry, len(shapes)),
        out_shape=jax.ShapeDtypeStruct((rows, width), jnp.float32),
        in_specs=[pl.BlockSpec(memory_space=pl.ANY)] * 2,
        out_specs=pl.BlockSpec(memory_space=pltpu.VMEM),
        scratch_shapes=[
            pltpu.VMEM((2, units, rows, half), jnp.bfloat16),
            pltpu.VMEM((units, 2, half, width), jnp.bfloat16),
            pltpu.VMEM((2, 2, rows, width), jnp.float32),
            pltpu.VMEM((2, rows, width), jnp.float32),
            pltpu.VMEM((rows, width), jnp.float32),
            pltpu.SemaphoreType.DMA((2,)),
            *sems,
        ],
        compiler_params=pltpu.CompilerParams(
            collective_id=0, has_side_effects=True, vmem_limit_bytes=63 * 1024 * 1024),
    )(left_sparse, right_sparse)
    kept = total.reshape(rows // BLOCK, BLOCK, width // BLOCK, BLOCK) * keep_mask[
        :, None, :, None
    ].astype(jnp.float32)
    return kept.reshape(rows, width).astype(jnp.bfloat16)


def solution(mesh):
    placed = (P("row", "col"), P("row", "col"), P("row", "col"), P("row", "col"), P("row", "col"))
    two_by_two = mesh.shape["row"] == TICKS + 1 and mesh.shape["col"] == 2 * mesh.shape["row"]
    return jax.shard_map(
        split_shards if two_by_two else shards, mesh=mesh, in_specs=placed, out_specs=P("row", "col"), check_vma=False
    )
```

```python
import functools

import jax
import jax.numpy as jnp
from jax import lax
from jax.experimental import pallas as pl
from jax.experimental.pallas import tpu as pltpu
from jax.sharding import PartitionSpec as P

BLOCK = 128
TICKS = 3


def passed_along(value, axis, by):
    length = lax.axis_size(axis)
    return lax.ppermute(value, axis, [(i, (i + by) % length) for i in range(length)])


def partner(block, axis, stride):
    count = lax.axis_size(axis)
    route = []
    for low in range(count):
        high = low | 1 << stride
        if high != low and high < count:
            route += [(low, high), (high, low)]
    return lax.ppermute(block, axis, route)


def sparsify(matrix, mask):
    rows, cols = matrix.shape
    shaped = matrix.reshape(rows // BLOCK, BLOCK, cols // BLOCK, BLOCK)
    return (shaped * mask[:, None, :, None].astype(matrix.dtype)).reshape(rows, cols)


def shards(left_matrix, right_matrix, left_mask, right_mask, keep_mask):
    row_index = lax.axis_index("row")
    col_index = lax.axis_index("col")
    group = col_index // 2
    parity = col_index % 2
    levels = lax.axis_size("row").bit_length() - 1
    left_sparse = sparsify(left_matrix, left_mask)
    right_sparse = sparsify(right_matrix, right_mask)

    def join(own, other):
        lower = jnp.where(parity == 0, own, other)
        upper = jnp.where(parity == 0, other, own)
        return jnp.concatenate([lower, upper], axis=1)

    for level in range(levels):
        moved = passed_along(right_sparse, "row", -(1 << level))
        right_sparse = jnp.where((group >> level) % 2 == 1, moved, right_sparse)
    holding = left_sparse
    for level in range(levels):
        moved = passed_along(holding, "col", -(2 << level))
        holding = jnp.where((row_index >> level) % 2 == 1, moved, holding)

    def whole(state):
        return join(state, partner(state, "col", 0))

    total = jnp.dot(whole(holding), right_sparse, preferred_element_type=jnp.float32)
    for tick in range(1, TICKS):
        holding = passed_along(holding, "col", -2)
        right_sparse = passed_along(right_sparse, "row", -1)
        total = total + jnp.dot(whole(holding), right_sparse, preferred_element_type=jnp.float32)
    rows, cols = total.shape
    kept = total.reshape(rows // BLOCK, BLOCK, cols // BLOCK, BLOCK) * keep_mask[
        :, None, :, None
    ].astype(jnp.float32)
    return kept.reshape(rows, cols).astype(jnp.bfloat16)


LEFT_PIECES = 4
RIGHT_PIECES = 4
SUM_PIECES = 4


def product_kernel(lsrc, rsrc, out, lbuf, rbuf, acc, core_sum, far_sum, via, loc, y_l, y_r, x_own, x_fwd, line, side, swap, sums):
    r, c = lax.axis_index("row"), lax.axis_index("col")
    y, x = r // 2, lax.rem(r, 2)
    z, p = c // 2, lax.rem(c, 2)
    rows, half = lbuf.shape[2:]
    width = rbuf.shape[3]
    lrows, rrows, srows = rows // LEFT_PIECES, half // RIGHT_PIECES, rows // SUM_PIECES
    ring = lbuf.shape[1]

    def device(dy, dx, dz, core):
        ny = 1 - y if dy else y
        nx = 1 - x if dx else x
        return (ny * 2 + nx, lax.rem(z + dz + ring, ring) * 2 + core)

    def unit_of(dy, dx):
        return (1 - y if dy else y) * 2 + (1 - x if dx else x)

    def copy(src, dst, sems, index, to):
        send, recv = sems
        return pltpu.make_async_remote_copy(
            src_ref=src, dst_ref=dst, send_sem=send.at[index], recv_sem=recv.at[index],
            device_id=to, device_id_type=pl.DeviceIdType.MESH)

    def arrived(dst, sems, index):
        copy(dst, dst, sems, index, device(0, 0, 0, 1 - p)).wait_recv()

    def used(panel, unit):
        return lax.rem(unit - (x + 2 * panel) - z + 2 * ring, ring) < TICKS

    barrier = pltpu.get_barrier_semaphore()
    peers = [device(1, 0, 0, 0), device(1, 0, 0, 1), device(0, 1, 0, 0), device(0, 1, 0, 1),
             device(0, 0, 0, 1 - p), device(0, 0, 1, p), device(0, 0, -1, p)]
    for peer in peers:
        pl.semaphore_signal(barrier, inc=1, device_id=peer, device_id_type=pl.DeviceIdType.MESH)
    pl.semaphore_wait(barrier, len(peers))

    pending = []

    def send(transfer, when=None):
        pending.append((transfer, when))
        if when is None:
            transfer.start()
        else:
            @pl.when(when)
            def _():
                transfer.start()

    def left_at(panel, unit, j):
        return lbuf.at[panel, unit, pl.ds(j * lrows, lrows)]

    def right_at(unit, q, j):
        return rbuf.at[unit, q, pl.ds(j * rrows, rrows)]

    def left_source(part, j):
        return lsrc.at[pl.ds(j * lrows, lrows), pl.ds(pl.multiple_of(part * half, 128), half)]

    def right_source(core, part, j):
        return rsrc.at[pl.ds(pl.multiple_of((core * 2 + part) * half + j * rrows, 128), rrows)]

    def needed(panel, d, at, unit):
        ok = False
        for step in range(ring):
            spot = at + step * d
            use = lax.rem(unit - (x + 2 * panel) - spot + 3 * ring, ring) < TICKS
            ok = ok | ((spot >= 0) & (spot < ring) & use)
        return ok & (unit >= 0) & (unit < ring)

    def comes(panel, d, m):
        return needed(panel, d, z, z - m * d) & (z - m * d >= 0) & (z - m * d < ring)

    def leaves(panel, d, m):
        return needed(panel, d, z + d, z - m * d) & ((m == 0) | comes(panel, d, m))

    def slot(panel, d, m, j):
        return (0 if d == -1 else 1, panel, m, j)

    def unit_back(d, m):
        return lax.clamp(0, z - m * d, ring - 1)

    def aside(d, panel, j):
        inner = ring - 2 if d == 1 else 1
        return (panel == 0) & (z == inner) & (j >= LEFT_PIECES // 2)

    def first_hop(panel_is_own, j):
        panel = y if panel_is_own else 1 - y
        src = left_source(y, j) if panel_is_own else left_at(panel, z, j)
        for d in (-1, 1):
            go = leaves(panel, d, 0)
            off = aside(d, panel, j) & (x == 1)
            send(copy(src, left_at(panel, z, j), line, slot(panel, d, 0, j), device(0, 0, d, p)), go & ~off)
            if j >= LEFT_PIECES // 2:
                send(copy(src, via.at[j - LEFT_PIECES // 2], side, (0, j), device(0, 1, 0, p)), go & off)

    def forward(panel, m, j):
        for d in (-1, 1):
            go = leaves(panel, d, m)
            unit = unit_back(d, m)
            @pl.when(go)
            def _():
                arrived(left_at(panel, unit, j), line, slot(panel, d, m - 1, j))
            send(copy(left_at(panel, unit, j), left_at(panel, unit, j), line, slot(panel, d, m, j), device(0, 0, d, p)), go)

    def settle(panel, m, j):
        for d in (-1, 1):
            @pl.when(comes(panel, d, m) & ~leaves(panel, d, m))
            def _():
                arrived(left_at(panel, unit_back(d, m), j), line, slot(panel, d, m - 1, j))

    def detour(j):
        hold = via.at[j - LEFT_PIECES // 2]
        for d in (-1, 1):
            inner = ring - 2 if d == 1 else 1
            here = (x == 0) & (z == inner)
            @pl.when(here)
            def _():
                arrived(hold, side, (0, j))
            send(copy(hold, hold, side, (1, j), device(0, 0, d, p)), here)

    def detour_back(j):
        hold = via.at[j - LEFT_PIECES // 2]
        for d in (-1, 1):
            inner = ring - 2 if d == 1 else 1
            end = inner + d
            there = (x == 0) & (z == end)
            @pl.when(there)
            def _():
                arrived(hold, side, (1, j))
            send(copy(hold, left_at(0, inner, j), line, slot(0, d, 0, j), device(0, 1, 0, p)), there)

    own_left = [pltpu.make_async_copy(lsrc.at[:, pl.ds(pl.multiple_of(y * half, 128), half)], lbuf.at[y, z], loc.at[0]),
                pltpu.make_async_copy(rsrc.at[pl.ds(pl.multiple_of((p * 2 + y) * half, 128), half)], rbuf.at[r, p], loc.at[1])]
    for j in range(LEFT_PIECES):
        send(copy(left_source(1 - y, j), left_at(y, z, j), y_l, (j,), device(1, 0, 0, p)))
        first_hop(True, j)
        if j < RIGHT_PIECES:
            for core in range(2):
                send(copy(right_source(core, y, j), right_at(r, p, j), x_own, (core, p, j), device(0, 1, 0, core)))
    send(copy(rsrc.at[pl.ds(pl.multiple_of(((1 - p) * 2 + y) * half, 128), half)], rbuf.at[r, p], swap, (0,), device(0, 0, 0, 1 - p)))
    for local in own_left:
        local.start()
    for j in range(RIGHT_PIECES):
        for core in range(2):
            send(copy(right_source(core, 1 - y, j), right_at(r, p, j), y_r, (core, p, j), device(1, 0, 0, core)))

    acc[...] = jnp.zeros_like(acc)

    behind = unit_of(1, 0)
    for j in range(LEFT_PIECES):
        arrived(left_at(1 - y, z, j), y_l, (j,))
        first_hop(False, j)
    for j in range(LEFT_PIECES):
        forward(1 - y, 1, j)
    for j in range(LEFT_PIECES // 2, LEFT_PIECES):
        detour(j)
    for j in range(RIGHT_PIECES):
        for q in range(2):
            arrived(right_at(behind, q, j), y_r, (p, q, j))
            send(copy(right_at(behind, q, j), right_at(behind, q, j), x_fwd, (q, j), device(0, 1, 0, p)))
    for j in range(LEFT_PIECES // 2, LEFT_PIECES):
        detour_back(j)
    for m, own in ((2, False), (1, True), (2, True)):
        for j in range(LEFT_PIECES):
            forward(y if own else 1 - y, m, j)

    def multiply(panel, unit, start, depth):
        @pl.when(used(panel, unit))
        def _():
            for q in range(2):
                acc[panel, q] += jnp.dot(
                    lbuf[panel, unit, :, start:start + depth], rbuf[unit, q, start:start + depth],
                    preferred_element_type=jnp.float32)

    for local in own_left:
        local.wait()
    arrived(rbuf.at[r, 1 - p], swap, (0,))
    across = unit_of(0, 1)
    for j in range(RIGHT_PIECES):
        for q in range(2):
            arrived(right_at(across, q, j), x_own, (p, q, j))
    for m in range(1, ring):
        for j in range(LEFT_PIECES):
            settle(1 - y, m, j)

    def early(panel):
        @pl.loop(0, 3)
        def _(step):
            unit = jnp.where(step == 0, r, jnp.where(step == 1, across, behind))
            multiply(panel, unit, 0, half)

    early(1 - y)
    last = unit_of(1, 1)
    for j in range(RIGHT_PIECES):
        for q in range(2):
            arrived(right_at(last, q, j), x_fwd, (q, j))
        multiply(1 - y, last, j * rrows, rrows)

    def part(ref, j, *index):
        return ref.at[(*index, pl.ds(j * srows, srows))]

    for j in range(SUM_PIECES):
        send(copy(part(acc, j, 1 - y, 1 - p), part(core_sum, j, 0), sums, (0, j), device(0, 0, 0, 1 - p)))
    for j in range(SUM_PIECES):
        piece = pl.ds(j * srows, srows)
        arrived(part(core_sum, j, 0), sums, (0, j))
        acc[1 - y, p, piece] += core_sum[0, piece]
        send(copy(part(acc, j, 1 - y, p), part(far_sum, j), sums, (1, j), device(1, 0, 0, p)))
    multiply(y, z, 0, half)
    for m in range(1, ring):
        for j in range(LEFT_PIECES):
            settle(y, m, j)
        for d in (-1, 1):
            @pl.when((z - m * d >= 0) & (z - m * d < ring))
            def _():
                multiply(y, unit_back(d, m), 0, half)
    for j in range(SUM_PIECES):
        send(copy(part(acc, j, y, 1 - p), part(core_sum, j, 1), sums, (2, j), device(0, 0, 0, 1 - p)))
    for j in range(SUM_PIECES):
        piece = pl.ds(j * srows, srows)
        arrived(part(core_sum, j, 1), sums, (2, j))
        arrived(part(far_sum, j), sums, (1, j))
        out[piece] = acc[y, p, piece] + core_sum[1, piece] + far_sum[piece]

    for transfer, when in pending:
        if when is None:
            transfer.wait_send()
        else:
            @pl.when(when)
            def _():
                transfer.wait_send()


def kernel_entry(sems, lsrc, rsrc, out, lbuf, rbuf, acc, core_sum, far_sum, via, loc, *rest):
    pairs = [(rest[2 * i], rest[2 * i + 1]) for i in range(sems)]
    product_kernel(lsrc, rsrc, out, lbuf, rbuf, acc, core_sum, far_sum, via, loc, *pairs)


def split_shards(left_matrix, right_matrix, left_mask, right_mask, keep_mask):
    left_sparse = sparsify(left_matrix, left_mask)
    right_sparse = sparsify(right_matrix, right_mask)
    rows, depth = left_matrix.shape
    width = right_matrix.shape[1]
    half = depth // 2
    units = lax.axis_size("row")
    shapes = [(LEFT_PIECES,), (2, 2, RIGHT_PIECES), (2, 2, RIGHT_PIECES), (2, RIGHT_PIECES),
              (2, 2, units - 1, LEFT_PIECES), (2, LEFT_PIECES), (1,), (3, SUM_PIECES)]
    sems = [pltpu.SemaphoreType.DMA(shape) for shape in shapes for _ in range(2)]
    total = pl.pallas_call(
        functools.partial(kernel_entry, len(shapes)),
        out_shape=jax.ShapeDtypeStruct((rows, width), jnp.float32),
        in_specs=[pl.BlockSpec(memory_space=pl.ANY)] * 2,
        out_specs=pl.BlockSpec(memory_space=pltpu.VMEM),
        scratch_shapes=[
            pltpu.VMEM((2, units, rows, half), jnp.bfloat16),
            pltpu.VMEM((units, 2, half, width), jnp.bfloat16),
            pltpu.VMEM((2, 2, rows, width), jnp.float32),
            pltpu.VMEM((2, rows, width), jnp.float32),
            pltpu.VMEM((rows, width), jnp.float32),
            pltpu.VMEM((LEFT_PIECES // 2, rows // LEFT_PIECES, half), jnp.bfloat16),
            pltpu.SemaphoreType.DMA((2,)),
            *sems,
        ],
        compiler_params=pltpu.CompilerParams(
            collective_id=0, has_side_effects=True, vmem_limit_bytes=63 * 1024 * 1024),
    )(left_sparse, right_sparse)
    kept = total.reshape(rows // BLOCK, BLOCK, width // BLOCK, BLOCK) * keep_mask[
        :, None, :, None
    ].astype(jnp.float32)
    return kept.reshape(rows, width).astype(jnp.bfloat16)


def solution(mesh):
    placed = (P("row", "col"), P("row", "col"), P("row", "col"), P("row", "col"), P("row", "col"))
    two_by_two = mesh.shape["row"] == TICKS + 1 and mesh.shape["col"] == 2 * mesh.shape["row"]
    return jax.shard_map(
        split_shards if two_by_two else shards, mesh=mesh, in_specs=placed, out_specs=P("row", "col"), check_vma=False
    )
```

```python
import functools

import jax
import jax.numpy as jnp
from jax import lax
from jax.experimental import pallas as pl
from jax.experimental.pallas import tpu as pltpu
from jax.sharding import PartitionSpec as P

BLOCK = 128
TICKS = 3


def passed_along(value, axis, by):
    length = lax.axis_size(axis)
    return lax.ppermute(value, axis, [(i, (i + by) % length) for i in range(length)])


def partner(block, axis, stride):
    count = lax.axis_size(axis)
    route = []
    for low in range(count):
        high = low | 1 << stride
        if high != low and high < count:
            route += [(low, high), (high, low)]
    return lax.ppermute(block, axis, route)


def sparsify(matrix, mask):
    rows, cols = matrix.shape
    shaped = matrix.reshape(rows // BLOCK, BLOCK, cols // BLOCK, BLOCK)
    return (shaped * mask[:, None, :, None].astype(matrix.dtype)).reshape(rows, cols)


def shards(left_matrix, right_matrix, left_mask, right_mask, keep_mask):
    row_index = lax.axis_index("row")
    col_index = lax.axis_index("col")
    group = col_index // 2
    parity = col_index % 2
    levels = lax.axis_size("row").bit_length() - 1
    left_sparse = sparsify(left_matrix, left_mask)
    right_sparse = sparsify(right_matrix, right_mask)

    def join(own, other):
        lower = jnp.where(parity == 0, own, other)
        upper = jnp.where(parity == 0, other, own)
        return jnp.concatenate([lower, upper], axis=1)

    for level in range(levels):
        moved = passed_along(right_sparse, "row", -(1 << level))
        right_sparse = jnp.where((group >> level) % 2 == 1, moved, right_sparse)
    holding = left_sparse
    for level in range(levels):
        moved = passed_along(holding, "col", -(2 << level))
        holding = jnp.where((row_index >> level) % 2 == 1, moved, holding)

    def whole(state):
        return join(state, partner(state, "col", 0))

    total = jnp.dot(whole(holding), right_sparse, preferred_element_type=jnp.float32)
    for tick in range(1, TICKS):
        holding = passed_along(holding, "col", -2)
        right_sparse = passed_along(right_sparse, "row", -1)
        total = total + jnp.dot(whole(holding), right_sparse, preferred_element_type=jnp.float32)
    rows, cols = total.shape
    kept = total.reshape(rows // BLOCK, BLOCK, cols // BLOCK, BLOCK) * keep_mask[
        :, None, :, None
    ].astype(jnp.float32)
    return kept.reshape(rows, cols).astype(jnp.bfloat16)


LEFT_PIECES = 4
RIGHT_PIECES = 4
SUM_PIECES = 4


def product_kernel(lsrc, rsrc, out, lbuf, rbuf, acc, core_sum, far_sum, via, loc, y_l, y_r, x_own, x_fwd, line, side, swap, sums):
    r, c = lax.axis_index("row"), lax.axis_index("col")
    y, x = r // 2, lax.rem(r, 2)
    z, p = c // 2, lax.rem(c, 2)
    rows, half = lbuf.shape[2:]
    width = rbuf.shape[3]
    lrows, rrows, srows = rows // LEFT_PIECES, half // RIGHT_PIECES, rows // SUM_PIECES
    ring = lbuf.shape[1]

    def device(dy, dx, dz, core):
        ny = 1 - y if dy else y
        nx = 1 - x if dx else x
        return (ny * 2 + nx, lax.rem(z + dz + ring, ring) * 2 + core)

    def unit_of(dy, dx):
        return (1 - y if dy else y) * 2 + (1 - x if dx else x)

    def copy(src, dst, sems, index, to):
        send, recv = sems
        return pltpu.make_async_remote_copy(
            src_ref=src, dst_ref=dst, send_sem=send.at[index], recv_sem=recv.at[index],
            device_id=to, device_id_type=pl.DeviceIdType.MESH)

    def arrived(dst, sems, index):
        copy(dst, dst, sems, index, device(0, 0, 0, 1 - p)).wait_recv()

    def used(panel, unit):
        return lax.rem(unit - (x + 2 * panel) - z + 2 * ring, ring) < TICKS

    barrier = pltpu.get_barrier_semaphore()
    peers = [device(1, 0, 0, 0), device(1, 0, 0, 1), device(0, 1, 0, 0), device(0, 1, 0, 1),
             device(0, 0, 0, 1 - p), device(0, 0, 1, p), device(0, 0, -1, p)]
    for peer in peers:
        pl.semaphore_signal(barrier, inc=1, device_id=peer, device_id_type=pl.DeviceIdType.MESH)
    pl.semaphore_wait(barrier, len(peers))

    pending = []

    def send(transfer, when=None):
        pending.append((transfer, when))
        if when is None:
            transfer.start()
        else:
            @pl.when(when)
            def _():
                transfer.start()

    def left_at(panel, unit, j):
        return lbuf.at[panel, unit, pl.ds(j * lrows, lrows)]

    def right_at(unit, q, j):
        return rbuf.at[unit, q, pl.ds(j * rrows, rrows)]

    def left_source(part, j):
        return lsrc.at[pl.ds(j * lrows, lrows), pl.ds(pl.multiple_of(part * half, 128), half)]

    def right_source(core, part, j):
        return rsrc.at[pl.ds(pl.multiple_of((core * 2 + part) * half + j * rrows, 128), rrows)]

    def needed(panel, d, at, unit):
        ok = False
        for step in range(ring):
            spot = at + step * d
            use = lax.rem(unit - (x + 2 * panel) - spot + 3 * ring, ring) < TICKS
            ok = ok | ((spot >= 0) & (spot < ring) & use)
        return ok & (unit >= 0) & (unit < ring)

    def comes(panel, d, m):
        return needed(panel, d, z, z - m * d) & (z - m * d >= 0) & (z - m * d < ring)

    def leaves(panel, d, m):
        return needed(panel, d, z + d, z - m * d) & ((m == 0) | comes(panel, d, m))

    def slot(panel, d, m, j):
        return (0 if d == -1 else 1, panel, m, j)

    def unit_back(d, m):
        return lax.clamp(0, z - m * d, ring - 1)

    def aside(d, panel, j):
        inner = ring - 2 if d == 1 else 1
        return (panel == 0) & (z == inner) & (j >= LEFT_PIECES // 2)

    def first_hop(panel_is_own, j):
        panel = y if panel_is_own else 1 - y
        src = left_source(y, j) if panel_is_own else left_at(panel, z, j)
        for d in (-1, 1):
            go = leaves(panel, d, 0)
            off = aside(d, panel, j) & (x == 1)
            send(copy(src, left_at(panel, z, j), line, slot(panel, d, 0, j), device(0, 0, d, p)), go & ~off)
            if j >= LEFT_PIECES // 2:
                send(copy(src, via.at[j - LEFT_PIECES // 2], side, (0, j), device(0, 1, 0, p)), go & off)

    def forward(panel, m, j):
        for d in (-1, 1):
            go = leaves(panel, d, m)
            unit = unit_back(d, m)
            @pl.when(go)
            def _():
                arrived(left_at(panel, unit, j), line, slot(panel, d, m - 1, j))
            send(copy(left_at(panel, unit, j), left_at(panel, unit, j), line, slot(panel, d, m, j), device(0, 0, d, p)), go)

    def settle(panel, m, j):
        for d in (-1, 1):
            @pl.when(comes(panel, d, m) & ~leaves(panel, d, m))
            def _():
                arrived(left_at(panel, unit_back(d, m), j), line, slot(panel, d, m - 1, j))

    def detour(j):
        hold = via.at[j - LEFT_PIECES // 2]
        for d in (-1, 1):
            inner = ring - 2 if d == 1 else 1
            here = (x == 0) & (z == inner)
            @pl.when(here)
            def _():
                arrived(hold, side, (0, j))
            send(copy(hold, hold, side, (1, j), device(0, 0, d, p)), here)

    def detour_back(j):
        hold = via.at[j - LEFT_PIECES // 2]
        for d in (-1, 1):
            inner = ring - 2 if d == 1 else 1
            end = inner + d
            there = (x == 0) & (z == end)
            @pl.when(there)
            def _():
                arrived(hold, side, (1, j))
            send(copy(hold, left_at(0, inner, j), line, slot(0, d, 0, j), device(0, 1, 0, p)), there)

    own_left = [pltpu.make_async_copy(lsrc.at[:, pl.ds(pl.multiple_of(y * half, 128), half)], lbuf.at[y, z], loc.at[0]),
                pltpu.make_async_copy(rsrc.at[pl.ds(pl.multiple_of((p * 2 + y) * half, 128), half)], rbuf.at[r, p], loc.at[1])]
    for j in range(LEFT_PIECES):
        send(copy(left_source(1 - y, j), left_at(y, z, j), y_l, (j,), device(1, 0, 0, p)))
        first_hop(True, j)
        if j < RIGHT_PIECES:
            for core in range(2):
                send(copy(right_source(core, y, j), right_at(r, p, j), x_own, (core, p, j), device(0, 1, 0, core)))
    send(copy(rsrc.at[pl.ds(pl.multiple_of(((1 - p) * 2 + y) * half, 128), half)], rbuf.at[r, p], swap, (0,), device(0, 0, 0, 1 - p)))
    for local in own_left:
        local.start()
    for j in range(RIGHT_PIECES):
        for core in range(2):
            send(copy(right_source(core, 1 - y, j), right_at(r, p, j), y_r, (core, p, j), device(1, 0, 0, core)))

    acc[...] = jnp.zeros_like(acc)

    behind = unit_of(1, 0)
    for j in range(LEFT_PIECES):
        arrived(left_at(1 - y, z, j), y_l, (j,))
        first_hop(False, j)
        forward(y, 1, j)
    for j in range(LEFT_PIECES):
        forward(1 - y, 1, j)
    for j in range(LEFT_PIECES // 2, LEFT_PIECES):
        detour(j)
    for j in range(RIGHT_PIECES):
        for q in range(2):
            arrived(right_at(behind, q, j), y_r, (p, q, j))
            send(copy(right_at(behind, q, j), right_at(behind, q, j), x_fwd, (q, j), device(0, 1, 0, p)))
    for j in range(LEFT_PIECES // 2, LEFT_PIECES):
        detour_back(j)
    for m, own in ((2, False), (2, True)):
        for j in range(LEFT_PIECES):
            forward(y if own else 1 - y, m, j)

    def multiply(panel, unit, start, depth):
        @pl.when(used(panel, unit))
        def _():
            for q in range(2):
                acc[panel, q] += jnp.dot(
                    lbuf[panel, unit, :, start:start + depth], rbuf[unit, q, start:start + depth],
                    preferred_element_type=jnp.float32)

    for local in own_left:
        local.wait()
    arrived(rbuf.at[r, 1 - p], swap, (0,))
    across = unit_of(0, 1)
    for j in range(RIGHT_PIECES):
        for q in range(2):
            arrived(right_at(across, q, j), x_own, (p, q, j))
    for m in range(1, ring):
        for j in range(LEFT_PIECES):
            settle(1 - y, m, j)

    def early(panel):
        @pl.loop(0, 3)
        def _(step):
            unit = jnp.where(step == 0, r, jnp.where(step == 1, across, behind))
            multiply(panel, unit, 0, half)

    early(1 - y)
    last = unit_of(1, 1)
    for j in range(RIGHT_PIECES):
        for q in range(2):
            arrived(right_at(last, q, j), x_fwd, (q, j))
        multiply(1 - y, last, j * rrows, rrows)

    def part(ref, j, *index):
        return ref.at[(*index, pl.ds(j * srows, srows))]

    for j in range(SUM_PIECES):
        send(copy(part(acc, j, 1 - y, 1 - p), part(core_sum, j, 0), sums, (0, j), device(0, 0, 0, 1 - p)))
    for j in range(SUM_PIECES):
        piece = pl.ds(j * srows, srows)
        arrived(part(core_sum, j, 0), sums, (0, j))
        acc[1 - y, p, piece] += core_sum[0, piece]
        send(copy(part(acc, j, 1 - y, p), part(far_sum, j), sums, (1, j), device(1, 0, 0, p)))
    multiply(y, z, 0, half)
    for m in range(1, ring):
        for j in range(LEFT_PIECES):
            settle(y, m, j)
        for d in (-1, 1):
            @pl.when((z - m * d >= 0) & (z - m * d < ring))
            def _():
                multiply(y, unit_back(d, m), 0, half)
    for j in range(SUM_PIECES):
        send(copy(part(acc, j, y, 1 - p), part(core_sum, j, 1), sums, (2, j), device(0, 0, 0, 1 - p)))
    for j in range(SUM_PIECES):
        piece = pl.ds(j * srows, srows)
        arrived(part(core_sum, j, 1), sums, (2, j))
        arrived(part(far_sum, j), sums, (1, j))
        out[piece] = acc[y, p, piece] + core_sum[1, piece] + far_sum[piece]

    for transfer, when in pending:
        if when is None:
            transfer.wait_send()
        else:
            @pl.when(when)
            def _():
                transfer.wait_send()


def kernel_entry(sems, lsrc, rsrc, out, lbuf, rbuf, acc, core_sum, far_sum, via, loc, *rest):
    pairs = [(rest[2 * i], rest[2 * i + 1]) for i in range(sems)]
    product_kernel(lsrc, rsrc, out, lbuf, rbuf, acc, core_sum, far_sum, via, loc, *pairs)


def split_shards(left_matrix, right_matrix, left_mask, right_mask, keep_mask):
    left_sparse = sparsify(left_matrix, left_mask)
    right_sparse = sparsify(right_matrix, right_mask)
    rows, depth = left_matrix.shape
    width = right_matrix.shape[1]
    half = depth // 2
    units = lax.axis_size("row")
    shapes = [(LEFT_PIECES,), (2, 2, RIGHT_PIECES), (2, 2, RIGHT_PIECES), (2, RIGHT_PIECES),
              (2, 2, units - 1, LEFT_PIECES), (2, LEFT_PIECES), (1,), (3, SUM_PIECES)]
    sems = [pltpu.SemaphoreType.DMA(shape) for shape in shapes for _ in range(2)]
    total = pl.pallas_call(
        functools.partial(kernel_entry, len(shapes)),
        out_shape=jax.ShapeDtypeStruct((rows, width), jnp.float32),
        in_specs=[pl.BlockSpec(memory_space=pl.ANY)] * 2,
        out_specs=pl.BlockSpec(memory_space=pltpu.VMEM),
        scratch_shapes=[
            pltpu.VMEM((2, units, rows, half), jnp.bfloat16),
            pltpu.VMEM((units, 2, half, width), jnp.bfloat16),
            pltpu.VMEM((2, 2, rows, width), jnp.float32),
            pltpu.VMEM((2, rows, width), jnp.float32),
            pltpu.VMEM((rows, width), jnp.float32),
            pltpu.VMEM((LEFT_PIECES // 2, rows // LEFT_PIECES, half), jnp.bfloat16),
            pltpu.SemaphoreType.DMA((2,)),
            *sems,
        ],
        compiler_params=pltpu.CompilerParams(
            collective_id=0, has_side_effects=True, vmem_limit_bytes=63 * 1024 * 1024),
    )(left_sparse, right_sparse)
    kept = total.reshape(rows // BLOCK, BLOCK, width // BLOCK, BLOCK) * keep_mask[
        :, None, :, None
    ].astype(jnp.float32)
    return kept.reshape(rows, width).astype(jnp.bfloat16)


def solution(mesh):
    placed = (P("row", "col"), P("row", "col"), P("row", "col"), P("row", "col"), P("row", "col"))
    two_by_two = mesh.shape["row"] == TICKS + 1 and mesh.shape["col"] == 2 * mesh.shape["row"]
    return jax.shard_map(
        split_shards if two_by_two else shards, mesh=mesh, in_specs=placed, out_specs=P("row", "col"), check_vma=False
    )
```
